512 devices in a mesh: row: 16 (over y, x), col: 32 (over z, core).
Axes of the slice: x: 4, y: 4, z: 16, core: 2. Of those that a mesh axis runs over, the one named last changes fastest.
Arguments:
- coords: float32 [3, 16384], replicated, may hold values from 0 to 1
- lengths: float32 [3], replicated, may hold values from 0.4 to 1.2
- pattern: int32 [32, 32], replicated, may hold values from 0 to 1, as said below
- blocks: int32 [32], replicated, may hold values from 0 to 31, each once
- inverses: float32 [2, 512, 512], replicated, as said below
- earlier: bfloat16 [16384, 1024], P('row'), may hold values from -0.29882812 to 0.29882812
Outputs:
- schur: float32 [16384, 16384], P('row', 'col')
The draws below stay inside these ranges and needn't reach their ends.
Inputs may be any that keep to these rules, and one draw needn't show every extreme that they name: `pattern`: symmetric, with ones on the diagonal. `blocks`: each tile gets its own site block. `inverses`: each of the two factors is lower triangular with a positive diagonal.
All inputs are finite; a program needn't handle non-finite values.
Results may differ from the reference program's by a relative error of at most 0.0007.
Values may be sent and summed in bfloat16 or wider, within the bound.
No kernel may reach another device: no remote copies, remote signals or barrier semaphores. Data moves between devices by JAX's collectives and lax.ppermute only.
A program may use at most 64 MiB of HBM per device.

```python
import math
import jax
import jax.numpy as jnp
from jax import lax

TB = 512
W = 1024
NT = 32
NSITE = 16384
N_ROW = 16
N_COL = 32


def draw_pattern(key, part):
    random_bits = jax.random.randint(jax.random.fold_in(key, 11), (NT, NT), 0, 2, dtype=jnp.int32)
    upper = jnp.triu(random_bits, 1)
    return (upper + upper.T + jnp.eye(NT, dtype=jnp.int32)).astype(jnp.int32)


def draw_inverses(key, part):
    off_key = jax.random.fold_in(key, 21)
    diag_key = jax.random.fold_in(key, 22)
    lower = jax.random.normal(off_key, (2, TB, TB), jnp.float32) * (0.1 / TB ** 0.5)
    diagonal = jax.random.uniform(diag_key, (2, TB), jnp.float32, 0.05, 0.15)
    eye_matrix = jnp.eye(TB, dtype=jnp.float32)
    return jnp.tril(lower, -1) + eye_matrix[None] * diagonal[:, None, :]


def steps_of(own_key, extent, shards, smallest, high):
    def one(dim, parts):
        draws = jax.random.uniform(jax.random.fold_in(jax.random.fold_in(own_key, 6), dim), (parts,), jnp.float32, smallest / len(shards), high / len(shards))
        return jnp.repeat(jnp.exp(draws), extent[dim] // parts).reshape((-1,) + (1,) * (len(extent) - dim - 1))

    factor_of = one(*shards[0])
    for cut in shards[1:]:
        factor_of = factor_of * one(*cut)
    return factor_of


def scatter_about(rng, dims, width, most, shards=(), kind=jnp.bfloat16):
    entries = width * jax.random.normal(rng, dims, jnp.float32)
    if shards:
        entries = entries * steps_of(rng, dims, shards, -0.22, 0.18)
    return jnp.clip(entries, -most, most).astype(kind)


def setup_inputs(seed: int = 0) -> dict:
    splits = jax.random.split(jax.random.key(seed), 7)
    coords = jnp.clip(jax.random.uniform(splits[0], (3, NSITE), jnp.float32, 0.0, 1.0), 0.0, 1.0)
    lengths = jnp.clip(jnp.exp(jax.random.uniform(splits[1], (3,), jnp.float32, math.log(0.4), math.log(1.2))), 0.4, 1.2)
    pattern = draw_pattern(jax.random.fold_in(splits[6], 71), 0)
    blocks = jax.random.permutation(splits[3], NT).astype(jnp.int32)
    inverses = draw_inverses(jax.random.fold_in(splits[6], 71), 0)
    earlier = scatter_about(splits[5], (NSITE, W), 0.05, 0.29882812, ((0, 16),))
    return {"coords": coords, "lengths": lengths, "pattern": pattern, "blocks": blocks, "inverses": inverses, "earlier": earlier}


def wendland(left_sites, right_sites):
    sq_dist = jnp.zeros((left_sites.shape[1], right_sites.shape[1]), jnp.float32)
    for component in range(3):
        offset = left_sites[component][:, None] - right_sites[component][None, :]
        sq_dist = sq_dist + offset * offset
    radius = jnp.sqrt(sq_dist)
    falloff = jnp.maximum(1.0 - radius, 0.0)
    return falloff ** 4 * (4.0 * radius + 1.0)

def outer_low(left_rows, right_rows):
    return lax.dot_general(left_rows, right_rows, (((1,), (1,)), ((), ())), preferred_element_type=jnp.float32)

def outer_high(left_rows, right_rows):
    return lax.dot_general(left_rows, right_rows, (((1,), (1,)), ((), ())), precision=lax.Precision.HIGHEST, preferred_element_type=jnp.float32)

def reference(coords, lengths, pattern, blocks, inverses, earlier):
    row_tiles_n = NT // N_ROW
    col_tiles_n = NT // N_COL
    positions = jnp.arange(NT, dtype=jnp.int32)
    row_order = positions % row_tiles_n * N_ROW + positions // row_tiles_n
    col_order = positions % col_tiles_n * N_COL + positions // col_tiles_n
    grouped = jnp.take(coords.reshape(3, NT, TB), blocks, axis=1) / lengths[:, None, None]
    row_sites = jnp.take(grouped, row_order, axis=1).reshape(3, NSITE)
    col_sites = jnp.take(grouped, col_order, axis=1).reshape(3, NSITE)
    patf = pattern.astype(jnp.float32)
    row_pattern = jnp.take(patf, row_order, axis=0)
    earlier_blocks = earlier.reshape(NT, TB, W)
    first_earlier = earlier_blocks[0]
    second_earlier = earlier_blocks[row_tiles_n]
    mask_first = jnp.repeat(row_pattern[:, 0], TB)
    mask_second = jnp.repeat(row_pattern[:, 1], TB)
    cov_first = wendland(row_sites, grouped[:, 0]) * mask_first[:, None]
    cov_first = cov_first - outer_low(earlier, first_earlier)
    first_panel = outer_high(cov_first, inverses[0])
    first_tile = first_panel[row_tiles_n * TB:row_tiles_n * TB + TB]
    cov_second = wendland(row_sites, grouped[:, 1]) * mask_second[:, None]
    cov_second = cov_second - outer_low(earlier, second_earlier) - outer_high(first_panel, first_tile)
    second_panel = outer_high(cov_second, inverses[1])
    col_pos = col_order % N_ROW * row_tiles_n + col_order // N_ROW
    col_earlier = jnp.take(earlier_blocks, col_pos, axis=0).reshape(NSITE, W)
    col_first = jnp.take(first_panel.reshape(NT, TB, TB), col_pos, axis=0).reshape(NSITE, TB)
    col_second = jnp.take(second_panel.reshape(NT, TB, TB), col_pos, axis=0).reshape(NSITE, TB)
    col_pattern = jnp.take(row_pattern, col_order, axis=1)

    def one_block(position):
        sites = lax.dynamic_slice_in_dim(row_sites, position * TB, TB, 1)
        mask_row = lax.dynamic_slice_in_dim(col_pattern, position, 1, 0)[0]
        cov = wendland(sites, col_sites).reshape(TB, NT, TB) * mask_row[None, :, None]
        cov = cov.reshape(TB, NSITE)
        rows_earlier = lax.dynamic_slice_in_dim(earlier, position * TB, TB, 0)
        rows_first = lax.dynamic_slice_in_dim(first_panel, position * TB, TB, 0)
        rows_second = lax.dynamic_slice_in_dim(second_panel, position * TB, TB, 0)
        return cov - outer_low(rows_earlier, col_earlier) - outer_high(rows_first, col_first) - outer_high(rows_second, col_second)
    schur = lax.map(one_block, positions)
    return schur.reshape(NSITE, NSITE)
```

```python
import jax
import jax.numpy as jnp
from jax import lax
from jax.experimental import pallas as pl
from jax.experimental.pallas import tpu as pltpu
from jax.sharding import PartitionSpec as P

TB = 512
VM = pl.BlockSpec(memory_space=pltpu.VMEM)
SM = pl.BlockSpec(memory_space=pltpu.SMEM)
LIMIT = 56 * 1024 * 1024


def dot_t(a, b):
    return lax.dot_general(a, b, (((1,), (1,)), ((), ())), preferred_element_type=jnp.float32)


def bf(a):
    return a.astype(jnp.bfloat16)


def halves(a):
    high = bf(a)
    return high, bf(a - high.astype(jnp.float32))


def dot3(a, b_high, b_low):
    a_high, a_low = halves(a)
    return dot_t(a_high, b_high) + (dot_t(a_low, b_high) + dot_t(a_high, b_low))


def wendland(left, right):
    sq_dist = None
    for component in range(3):
        offset = left[:, component : component + 1] - right[component : component + 1, :]
        sq_dist = offset * offset if sq_dist is None else sq_dist + offset * offset
    radius = jnp.sqrt(sq_dist)
    falloff = jnp.maximum(1.0 - radius, 0.0)
    falloff = falloff * falloff
    return falloff * falloff * (4.0 * radius + 1.0)


def cov_kernel(row_tiles_n, row_count):
    def body(ids, lengths, pattern, blocks, coords, cov_schur, cov_rows, cov_cols, cov_first):
        row_index = ids[0]
        col_tile = ids[1]

        def sites(tile):
            start = pl.multiple_of(blocks[tile] * TB, TB)
            return [coords[c : c + 1, pl.ds(start, TB)] / lengths[c] for c in range(3)]

        def as_rows(parts):
            return jnp.concatenate(parts, axis=0)

        def as_columns(parts):
            padded = jnp.concatenate(parts + [jnp.zeros((5, TB), jnp.float32)], axis=0)
            return padded.T

        panels = [as_rows(sites(0)), as_rows(sites(1))]
        column = sites(col_tile)
        column_rows = as_rows(column)
        column_left = as_columns(column)

        def put(ref, at, to, left, right, i, j):
            kept = pattern[i, j].astype(jnp.float32)
            for s in range(0, TB, 64):
                ref[at + s : at + s + 64, to : to + TB] = wendland(left[s : s + 64], right) * kept

        for slot in range(row_tiles_n):
            tile = slot * row_count + row_index
            left = as_columns(sites(tile))
            put(cov_schur, slot * TB, 0, left, column_rows, tile, col_tile)
            for p in range(2):
                put(cov_rows, slot * TB, p * TB, left, panels[p], tile, p)
        for p in range(2):
            put(cov_cols, 0, p * TB, column_left, panels[p], col_tile, p)
        put(cov_first, 0, 0, as_columns(sites(1)), panels[0], 1, 0)

    return body


def rows_kernel(ids, own, other, rows, cov_rows, cov_first, inverses, first, second, first_tile, panel_earlier):
    core = ids[2]
    panel_earlier[pl.ds(pl.multiple_of((1 - core) * TB, TB), TB), :] = own[...].reshape(TB, -1)
    panel_earlier[pl.ds(pl.multiple_of(core * TB, TB), TB), :] = other[...].reshape(TB, -1)
    zero = panel_earlier[:TB]
    one = panel_earlier[TB:]
    inv0_high, inv0_low = halves(inverses[0])
    inv1_high, inv1_low = halves(inverses[1])
    tile = bf(dot3(cov_first[...] - dot_t(one, zero), inv0_high, inv0_low))
    first_tile[...] = tile
    for s in range(0, rows.shape[0], TB):
        block = rows[s : s + TB]
        got = bf(dot3(cov_rows[s : s + TB, :TB] - dot_t(block, zero), inv0_high, inv0_low))
        first[s : s + TB] = got
        rest = cov_rows[s : s + TB, TB:] - dot_t(block, one) - dot_t(got, tile)
        second[s : s + TB] = bf(dot3(rest, inv1_high, inv1_low))


def tail_kernel(column, rows, panel_earlier, cov_schur, cov_cols, inverses, first, second, first_tile, out):
    mine = column[...].reshape(TB, -1)
    both = cov_cols[...] - dot_t(mine, panel_earlier[...])
    inv0_high, inv0_low = halves(inverses[0])
    inv1_high, inv1_low = halves(inverses[1])
    col_first = bf(dot3(both[:, :TB], inv0_high, inv0_low))
    rest = both[:, TB:] - dot_t(col_first, first_tile[...])
    col_second = bf(dot3(rest, inv1_high, inv1_low))
    for s in range(0, rows.shape[0], TB):
        out[s : s + TB] = (
            cov_schur[s : s + TB]
            - dot_t(rows[s : s + TB], mine)
            - dot_t(first[s : s + TB], col_first)
            - dot_t(second[s : s + TB], col_second)
        )


def call(body, outs, specs, **kw):
    return pl.pallas_call(
        body,
        out_shape=outs,
        in_specs=specs,
        out_specs=[VM] * len(outs) if isinstance(outs, (list, tuple)) else VM,
        compiler_params=pltpu.CompilerParams(vmem_limit_bytes=LIMIT),
        **kw,
    )


def local(coords, lengths, pattern, blocks, inverses, earlier):
    row_count = lax.axis_size("row")
    row_index = lax.axis_index("row")
    col_index = lax.axis_index("col")
    core = col_index % 2
    rows_n, width = earlier.shape
    row_tiles_n = rows_n // TB
    piece = TB // row_count
    f32 = jnp.float32
    ids = jnp.stack([row_index, col_index, core]).astype(jnp.int32)
    holder = col_index % row_count
    start = jnp.where(row_index == holder, col_index // row_count * TB, 0)
    mine = lax.dynamic_slice_in_dim(earlier, start, TB, 0).reshape(row_count, piece, width)
    scattered = lax.all_to_all(mine, "row", 0, 0)
    cov_schur, cov_rows, cov_cols, cov_first = call(
        cov_kernel(row_tiles_n, row_count),
        [
            jax.ShapeDtypeStruct((rows_n, TB), f32),
            jax.ShapeDtypeStruct((rows_n, 2 * TB), f32),
            jax.ShapeDtypeStruct((TB, 2 * TB), f32),
            jax.ShapeDtypeStruct((TB, TB), f32),
        ],
        [SM, SM, SM, SM, VM],
        name="cov",
    )(ids, lengths, pattern, blocks, coords)

    def gathered(source):
        part = lax.dynamic_index_in_dim(scattered, source, 0, keepdims=True)
        return lax.all_to_all(jnp.broadcast_to(part, scattered.shape), "row", 0, 0)

    own = gathered(1 - core)
    column = gathered(holder)
    other = lax.ppermute(own, "col", [(c, c ^ 1) for c in range(lax.axis_size("col"))])
    bf16 = jnp.bfloat16
    first, second, first_tile, panel_earlier = call(
        rows_kernel,
        [
            jax.ShapeDtypeStruct((rows_n, TB), bf16),
            jax.ShapeDtypeStruct((rows_n, TB), bf16),
            jax.ShapeDtypeStruct((TB, TB), bf16),
            jax.ShapeDtypeStruct((2 * TB, width), bf16),
        ],
        [SM] + [VM] * 6,
        name="rows",
    )(ids, own, other, earlier, cov_rows, cov_first, inverses)
    return call(tail_kernel, jax.ShapeDtypeStruct((rows_n, TB), f32), [VM] * 9, name="tail")(
        column, earlier, panel_earlier, cov_schur, cov_cols, inverses, first, second, first_tile
    )


def solution(mesh):
    return jax.shard_map(
        local,
        mesh=mesh,
        in_specs=(P(), P(), P(), P(), P(), P("row", None)),
        out_specs=P("row", "col"),
        check_vma=False,
    )
```

```python
import jax
import jax.numpy as jnp
from jax import lax
from jax.experimental import pallas as pl
from jax.experimental.pallas import tpu as pltpu
from jax.sharding import PartitionSpec as P


TB = 512
VM = pl.BlockSpec(memory_space=pltpu.VMEM)
SM = pl.BlockSpec(memory_space=pltpu.SMEM)
HB = pl.BlockSpec(memory_space=pl.ANY)
F32 = jnp.float32
BF16 = jnp.bfloat16


def dot_t(a, b):
    return lax.dot_general(a, b, (((1,), (1,)), ((), ())), preferred_element_type=F32)


def bf(a):
    return a.astype(BF16)


def halves(a):
    high = bf(a)
    return high, bf(a - high.astype(F32))


def dot3(a, b_high, b_low):
    a_high, a_low = halves(a)
    return dot_t(a_high, b_high) + (dot_t(a_low, b_high) + dot_t(a_high, b_low))


def wendland(left, right):
    sq_dist = None
    for component in range(3):
        offset = left[:, component : component + 1] - right[component : component + 1, :]
        sq_dist = offset * offset if sq_dist is None else sq_dist + offset * offset
    radius = jnp.sqrt(sq_dist)
    falloff = jnp.maximum(1.0 - radius, 0.0)
    falloff = falloff * falloff
    return falloff * falloff * (4.0 * radius + 1.0)


def sites(tile, lengths, blocks, coords):
    start = pl.multiple_of(blocks[tile] * TB, TB)
    return jnp.concatenate([coords[c : c + 1, pl.ds(start, TB)] / lengths[c] for c in range(3)], axis=0)


def as_columns(parts):
    return jnp.concatenate([parts, jnp.zeros((5, TB), F32)], axis=0).T


def put(ref, at, to, left, right, kept):
    for s in range(0, TB, 64):
        ref[at + s : at + s + 64, to : to + TB] = wendland(left[s : s + 64], right) * kept.astype(F32)


def panels_kernel(row_tiles_n, row_count):
    def body(ids, lengths, pattern, blocks, coords, inverses, cov_rows, cov_cols, cov_first, inv_high, inv_low):
        panels = [sites(p, lengths, blocks, coords) for p in range(2)]
        for slot in range(row_tiles_n):
            tile = slot * row_count + ids[0]
            left = as_columns(sites(tile, lengths, blocks, coords))
            for p in range(2):
                put(cov_rows, slot * TB, p * TB, left, panels[p], pattern[tile, p])
        left = as_columns(sites(ids[1], lengths, blocks, coords))
        for p in range(2):
            put(cov_cols, 0, p * TB, left, panels[p], pattern[ids[1], p])
        put(cov_first, 0, 0, as_columns(panels[1]), panels[0], pattern[1, 0])
        for p in range(2):
            inv_high[p], inv_low[p] = halves(inverses[p])

    return body


def schur_kernel(row_tiles_n, row_count):
    def body(ids, lengths, pattern, blocks, coords, cov_schur):
        right = sites(ids[1], lengths, blocks, coords)
        for slot in range(row_tiles_n):
            tile = slot * row_count + ids[0]
            left = as_columns(sites(tile, lengths, blocks, coords))
            put(cov_schur, slot * TB, 0, left, right, pattern[tile, ids[1]])

    return body


def fetch(pairs, sems):
    copies = [pltpu.make_async_copy(source, to, sems.at[n]) for n, (source, to) in enumerate(pairs)]
    for copy in copies:
        copy.start()
    return copies


def panel_parts(own, other, panels, core):
    return [(own, panels.at[1 - core]), (other, panels.at[core])]


def rows_kernel(
    ids, own, other, earlier, cov_rows_in, cov_first_in, inv_high_in, inv_low_in, first, second, first_tile,
    panels, rows, cov_rows, cov_first, inv_high, inv_low, sems,
):
    pairs = panel_parts(own, other, panels, ids[2])
    pairs += [(cov_first_in, cov_first), (inv_high_in, inv_high), (inv_low_in, inv_low)]
    pairs += [(earlier, rows), (cov_rows_in, cov_rows)]
    copies = fetch(pairs, sems)
    for copy in copies[:-2]:
        copy.wait()
    zero = panels[0].reshape(TB, -1)
    one = panels[1].reshape(TB, -1)
    inv0 = inv_high[0], inv_low[0]
    inv1 = inv_high[1], inv_low[1]
    tile = bf(dot3(cov_first[...] - dot_t(one, zero), *inv0))
    first_tile[...] = tile
    for copy in copies[-2:]:
        copy.wait()
    for s in range(0, rows.shape[0], TB):
        block = rows[s : s + TB]
        got = bf(dot3(cov_rows[s : s + TB, :TB] - dot_t(block, zero), *inv0))
        first[s : s + TB] = got
        rest = cov_rows[s : s + TB, TB:] - dot_t(block, one) - dot_t(got, tile)
        second[s : s + TB] = bf(dot3(rest, *inv1))


def tail_kernel(chunk):
    def body(
        ids, column_in, own, other, earlier, cov_schur_in, cov_cols_in, inv_high_in, first_in, second_in,
        first_tile_in, out,
        column, panels, rows, cov_schur, cov_cols, inv_high, first, second, first_tile, result, sems, out_sems,
    ):
        pairs = [(column_in, column), (earlier, rows), (cov_schur_in, cov_schur)]
        pairs += panel_parts(own, other, panels, ids[2])
        pairs += [(cov_cols_in, cov_cols), (inv_high_in, inv_high)]
        pairs += [(first_tile_in, first_tile), (first_in, first), (second_in, second)]
        copies = fetch(pairs, sems)
        steps = [pl.ds(s, chunk) for s in range(0, rows.shape[0], chunk)]
        for copy in copies[:3]:
            copy.wait()
        mine = column[...].reshape(TB, -1)
        for at in steps:
            result[at] = cov_schur[at] - dot_t(rows[at], mine)
        for copy in copies[3:-3]:
            copy.wait()
        start = cov_cols[:, :TB] - dot_t(mine, panels[0].reshape(TB, -1))
        rest = cov_cols[:, TB:] - dot_t(mine, panels[1].reshape(TB, -1))
        col_first = bf(dot_t(bf(start), inv_high[0]))
        for copy in copies[-3:]:
            copy.wait()
        rest = rest - dot_t(col_first, first_tile[...])
        col_second = bf(dot_t(bf(rest), inv_high[1]))
        outs = []
        for n, at in enumerate(steps):
            result[at] = result[at] - dot_t(first[at], col_first) - dot_t(second[at], col_second)
            outs.append(pltpu.make_async_copy(result.at[at], out.at[at], out_sems.at[n]))
            outs[-1].start()
        for copy in outs:
            copy.wait()

    return body


def call(body, outs, specs, out_specs=None, limit=63, **kw):
    return pl.pallas_call(
        body,
        out_shape=outs,
        in_specs=specs,
        out_specs=out_specs or [VM] * len(outs),
        compiler_params=pltpu.CompilerParams(vmem_limit_bytes=limit * 1024 * 1024),
        **kw,
    )


def steps(coords, lengths, pattern, blocks, inverses, earlier):
    row_count = lax.axis_size("row")
    col_count = lax.axis_size("col")
    row_index = lax.axis_index("row")
    col_index = lax.axis_index("col")
    core = col_index % 2
    rows_n, width = earlier.shape
    row_tiles_n = rows_n // TB
    piece = TB // row_count
    ids = jnp.stack([row_index, col_index, core]).astype(jnp.int32)

    holder = col_index % row_count
    start = jnp.where(row_index == holder, col_index // row_count * TB, 0)
    mine = lax.dynamic_slice_in_dim(earlier, start, TB, 0).reshape(row_count, piece, width)
    scattered = lax.all_to_all(mine, "row", 0, 0)

    (cov_schur,) = call(
        schur_kernel(row_tiles_n, row_count),
        [jax.ShapeDtypeStruct((rows_n, TB), F32)],
        [SM, SM, SM, SM, VM],
        name="schur",
    )(ids, lengths, pattern, blocks, coords)
    cov_rows, cov_cols, cov_first, inv_high, inv_low = call(
        panels_kernel(row_tiles_n, row_count),
        [
            jax.ShapeDtypeStruct((rows_n, 2 * TB), F32),
            jax.ShapeDtypeStruct((TB, 2 * TB), F32),
            jax.ShapeDtypeStruct((TB, TB), F32),
            jax.ShapeDtypeStruct((2, TB, TB), BF16),
            jax.ShapeDtypeStruct((2, TB, TB), BF16),
        ],
        [SM, SM, SM, SM, VM, VM],
        name="panels",
    )(ids, lengths, pattern, blocks, coords, inverses)
    panel_piece = lax.dynamic_index_in_dim(scattered, 1 - core, 0, keepdims=True)
    column_piece = lax.dynamic_index_in_dim(scattered, holder, 0, keepdims=True)
    panel_piece, column_piece, cov_schur, cov_rows = lax.optimization_barrier(
        (panel_piece, column_piece, cov_schur, cov_rows)
    )
    own = lax.all_to_all(jnp.broadcast_to(panel_piece, scattered.shape), "row", 0, 0)
    other = lax.ppermute(own, "col", [(c, c ^ 1) for c in range(col_count)])
    column = lax.all_to_all(jnp.broadcast_to(column_piece, scattered.shape), "row", 0, 0)
    panels = pltpu.VMEM((2,) + own.shape, BF16)
    square = pltpu.VMEM((TB, TB), BF16)
    pair = pltpu.VMEM((2, TB, TB), BF16)
    tall = pltpu.VMEM((rows_n, TB), BF16)
    whole = pltpu.VMEM(earlier.shape, BF16)
    block = pltpu.VMEM((rows_n, TB), F32)
    wide = pltpu.VMEM((TB, 2 * TB), F32)
    dma = pltpu.SemaphoreType.DMA
    first, second, first_tile = call(
        rows_kernel,
        [
            jax.ShapeDtypeStruct((rows_n, TB), BF16),
            jax.ShapeDtypeStruct((rows_n, TB), BF16),
            jax.ShapeDtypeStruct((TB, TB), BF16),
        ],
        [SM] + [HB] * 7,
        scratch_shapes=[
            panels, whole, pltpu.VMEM((rows_n, 2 * TB), F32), pltpu.VMEM((TB, TB), F32), pair, pair, dma((7,)),
        ],
        name="rows",
    )(ids, own, other, earlier, cov_rows, cov_first, inv_high, inv_low)
    chunk = 256
    return call(
        tail_kernel(chunk),
        jax.ShapeDtypeStruct((rows_n, TB), F32),
        [SM] + [HB] * 10,
        HB,
        scratch_shapes=[
            pltpu.VMEM(column.shape, BF16), panels, whole, block, wide, pair, tall, tall, square, block,
            dma((10,)), dma((rows_n // chunk,)),
        ],
        name="tail",
    )(ids, column, own, other, earlier, cov_schur, cov_cols, inv_high, first, second, first_tile)


def solution(mesh):
    return jax.shard_map(
        steps,
        mesh=mesh,
        in_specs=(P(), P(), P(), P(), P(), P("row", None)),
        out_specs=P("row", "col"),
        check_vma=False,
    )
```

```python
import jax
import jax.numpy as jnp
from jax import lax
from jax.experimental import pallas as pl
from jax.experimental.pallas import tpu as pltpu
from jax.sharding import PartitionSpec as P


TB = 512
VM = pl.BlockSpec(memory_space=pltpu.VMEM)
SM = pl.BlockSpec(memory_space=pltpu.SMEM)
HB = pl.BlockSpec(memory_space=pl.ANY)
F32 = jnp.float32
BF16 = jnp.bfloat16


def dot_t(a, b):
    return lax.dot_general(a, b, (((1,), (1,)), ((), ())), preferred_element_type=F32)


def bf(a):
    return a.astype(BF16)


def wendland(left, right):
    sq_dist = None
    for component in range(3):
        offset = left[:, component : component + 1] - right[component : component + 1, :]
        sq_dist = offset * offset if sq_dist is None else sq_dist + offset * offset
    radius = jnp.sqrt(sq_dist)
    falloff = jnp.maximum(1.0 - radius, 0.0)
    falloff = falloff * falloff
    return falloff * falloff * (4.0 * radius + 1.0)


def sites(tile, lengths, blocks, coords):
    start = pl.multiple_of(blocks[tile] * TB, TB)
    return jnp.concatenate([coords[c : c + 1, pl.ds(start, TB)] / lengths[c] for c in range(3)], axis=0)


def as_columns(parts):
    return jnp.concatenate([parts, jnp.zeros((5, TB), F32)], axis=0).T


def put(ref, at, to, left, right, kept):
    for s in range(0, TB, 64):
        ref[at + s : at + s + 64, to : to + TB] = wendland(left[s : s + 64], right) * kept.astype(F32)


def panels_kernel(row_tiles_n, row_count):
    def body(lengths, pattern, blocks, coords, inverses, cov_rows, cov_cols, cov_first, inverse):
        place_row, col_tile = place()
        panels = [sites(p, lengths, blocks, coords) for p in range(2)]
        for slot in range(row_tiles_n):
            tile = slot * row_count + place_row
            left = as_columns(sites(tile, lengths, blocks, coords))
            for p in range(2):
                put(cov_rows, slot * TB, p * TB, left, panels[p], pattern[tile, p])
        left = as_columns(sites(col_tile, lengths, blocks, coords))
        for p in range(2):
            put(cov_cols, 0, p * TB, left, panels[p], pattern[col_tile, p])
        put(cov_first, 0, 0, as_columns(panels[1]), panels[0], pattern[1, 0])
        for p in range(2):
            inverse[p] = bf(inverses[p])

    return body


def schur_kernel(row_tiles_n, row_count):
    def body(lengths, pattern, blocks, coords, cov_schur):
        place_row, col_tile = place()
        right = sites(col_tile, lengths, blocks, coords)
        for slot in range(row_tiles_n):
            tile = slot * row_count + place_row
            left = as_columns(sites(tile, lengths, blocks, coords))
            put(cov_schur, slot * TB, 0, left, right, pattern[tile, col_tile])

    return body


def fetch(pairs, sems):
    copies = [pltpu.make_async_copy(source, to, sems.at[n]) for n, (source, to) in enumerate(pairs)]
    for copy in copies:
        copy.start()
    return copies


def place():
    row = lax.axis_index("row")
    col = lax.axis_index("col")
    return row, col


def pack_kernel(parts):
    def body(earlier, out, sems):
        row, col = place()
        count = out.shape[0]
        start = jnp.where(row == col % count, col // count * count, 0)
        each = count // parts
        pairs = [(earlier.at[pl.ds(start + n * each, each)], out.at[pl.ds(n * each, each)]) for n in range(parts)]
        for copy in fetch(pairs, sems):
            copy.wait()

    return body


def spread_kernel(scattered, out, pieces, sems, out_sems):
    _, col = place()
    count = out.shape[0]
    pairs = [(scattered.at[1 - col % 2], pieces.at[0]), (scattered.at[col % count], pieces.at[1])]
    for copy in fetch(pairs, sems):
        copy.wait()
    for copy in fetch([(pieces, out.at[n]) for n in range(count)], out_sems):
        copy.wait()


def split_kernel(gathered, out, sems):
    each = out.shape[0] // 4
    steps = [pl.ds(n * each, each) for n in range(4)]
    for copy in fetch([(gathered.at[at, 0], out.at[at]) for at in steps], sems):
        copy.wait()


def early_kernel(chunk):
    def body(mine_in, earlier, cov_in, out, mine, rows, cov, result, sems, out_sems):
        steps = [pl.ds(s, chunk) for s in range(0, rows.shape[0], chunk)]
        pairs = [(mine_in.at[:, 1], mine)]
        for at in steps:
            pairs += [(earlier.at[at], rows.at[at]), (cov_in.at[at], cov.at[at])]
        copies = fetch(pairs, sems)
        copies[0].wait()
        column = mine[...].reshape(TB, -1)
        outs = []
        for n, at in enumerate(steps):
            copies[1 + 2 * n].wait()
            copies[2 + 2 * n].wait()
            result[at] = cov[at] - dot_t(rows[at], column)
            outs.append(pltpu.make_async_copy(result.at[at], out.at[at], out_sems.at[n]))
            outs[-1].start()
        for copy in outs:
            copy.wait()

    return body


def final_kernel(chunk):
    def body(
        mine_in, other_in, earlier, early_in, cov_rows_in, cov_cols_in, cov_first_in, inverse_in, out,
        mine, panels, rows, early, cov_rows, cov_cols, cov_first, inverse, sems, out_sems,
    ):
        core = place()[1] % 2
        pairs = [(mine_in.at[:, 0], panels.at[1 - core]), (other_in, panels.at[core])]
        pairs += [(mine_in.at[:, 1], mine), (cov_first_in, cov_first), (inverse_in, inverse), (cov_cols_in, cov_cols)]
        steps = [pl.ds(s, chunk) for s in range(0, rows.shape[0], chunk)]
        for at in steps:
            pairs += [(earlier.at[at], rows.at[at]), (cov_rows_in.at[at], cov_rows.at[at])]
        pairs += [(early_in.at[at], early.at[at]) for at in steps]
        copies = fetch(pairs, sems)
        for copy in copies[:3]:
            copy.wait()
        column = mine[...].reshape(TB, -1)
        zero = panels[0].reshape(TB, -1)
        one = panels[1].reshape(TB, -1)
        tile = dot_t(one, zero)
        start = dot_t(column, zero)
        rest = dot_t(column, one)
        for copy in copies[3:6]:
            copy.wait()
        tile = bf(dot_t(bf(cov_first[...] - tile), inverse[0]))
        col_first = bf(dot_t(bf(cov_cols[:, :TB] - start), inverse[0]))
        col_second = bf(dot_t(bf(cov_cols[:, TB:] - rest - dot_t(col_first, tile)), inverse[1]))
        outs = []
        for n, at in enumerate(steps):
            for copy in (*copies[6 + 2 * n : 8 + 2 * n], copies[6 + 2 * len(steps) + n]):
                copy.wait()
            block = rows[at]
            first = bf(dot_t(bf(cov_rows[at, :TB] - dot_t(block, zero)), inverse[0]))
            second = cov_rows[at, TB:] - dot_t(block, one) - dot_t(first, tile)
            second = bf(dot_t(bf(second), inverse[1]))
            early[at] = early[at] - dot_t(first, col_first) - dot_t(second, col_second)
            outs.append(pltpu.make_async_copy(early.at[at], out.at[at], out_sems.at[n]))
            outs[-1].start()
        for copy in outs:
            copy.wait()

    return body


def call(body, outs, specs, out_specs=None, limit=63, **kw):
    return pl.pallas_call(
        body,
        out_shape=outs,
        in_specs=specs,
        out_specs=out_specs or [VM] * len(outs),
        compiler_params=pltpu.CompilerParams(vmem_limit_bytes=limit * 1024 * 1024),
        **kw,
    )


def steps(coords, lengths, pattern, blocks, inverses, earlier):
    row_count = lax.axis_size("row")
    col_count = lax.axis_size("col")
    rows_n, width = earlier.shape
    row_tiles_n = rows_n // TB
    piece = TB // row_count
    dma = pltpu.SemaphoreType.DMA

    pieces = (row_count, piece, width)
    mine = call(pack_kernel(4), jax.ShapeDtypeStruct(pieces, BF16), [HB], HB, scratch_shapes=[dma((4,))], name="pack")(
        earlier.reshape(-1, piece, width)
    )
    scattered = lax.all_to_all(mine, "row", 0, 0)
    (cov_schur,) = call(
        schur_kernel(row_tiles_n, row_count),
        [jax.ShapeDtypeStruct((rows_n, TB), F32)],
        [SM, SM, SM, VM],
        name="schur",
    )(lengths, pattern, blocks, coords)
    scattered, cov_schur, later = lax.optimization_barrier((scattered, cov_schur, lengths))
    spread = call(
        spread_kernel,
        jax.ShapeDtypeStruct((row_count, 2, piece, width), BF16),
        [HB],
        HB,
        63,
        scratch_shapes=[pltpu.VMEM((2, piece, width), BF16), dma((2,)), dma((row_count,))],
        name="spread",
    )(scattered)
    gathered = lax.all_to_all(spread, "row", 0, 0)
    cov_rows, cov_cols, cov_first, inverse = call(
        panels_kernel(row_tiles_n, row_count),
        [
            jax.ShapeDtypeStruct((rows_n, 2 * TB), F32),
            jax.ShapeDtypeStruct((TB, 2 * TB), F32),
            jax.ShapeDtypeStruct((TB, TB), F32),
            jax.ShapeDtypeStruct((2, TB, TB), BF16),
        ],
        [SM, SM, SM, VM, VM],
        name="panels",
    )(later, pattern, blocks, coords, inverses)
    gathered, cov_rows = lax.optimization_barrier((gathered, cov_rows))
    own = call(split_kernel, jax.ShapeDtypeStruct(pieces, BF16), [HB], HB, scratch_shapes=[dma((4,))], name="split")(
        gathered
    )
    other = lax.ppermute(own, "col", [(c, c ^ 1) for c in range(col_count)])
    chunk = 256
    count = rows_n // chunk
    mine_buffer = pltpu.VMEM(pieces, BF16)
    whole = pltpu.VMEM(earlier.shape, BF16)
    block = pltpu.VMEM((rows_n, TB), F32)
    early = call(
        early_kernel(chunk),
        jax.ShapeDtypeStruct((rows_n, TB), F32),
        [HB] * 3,
        HB,
        scratch_shapes=[mine_buffer, whole, block, block, dma((1 + 2 * count,)), dma((count,))],
        name="early",
    )(gathered, earlier, cov_schur)
    other, early = lax.optimization_barrier((other, early))
    return call(
        final_kernel(chunk),
        jax.ShapeDtypeStruct((rows_n, TB), F32),
        [HB] * 8,
        HB,
        scratch_shapes=[
            mine_buffer,
            pltpu.VMEM((2,) + pieces, BF16),
            whole,
            block,
            pltpu.VMEM((rows_n, 2 * TB), F32),
            pltpu.VMEM((TB, 2 * TB), F32),
            pltpu.VMEM((TB, TB), F32),
            pltpu.VMEM((2, TB, TB), BF16),
            dma((6 + 3 * count,)),
            dma((count,)),
        ],
        name="final",
    )(gathered, other, earlier, early, cov_rows, cov_cols, cov_first, inverse)


def solution(mesh):
    return jax.shard_map(
        steps,
        mesh=mesh,
        in_specs=(P(), P(), P(), P(), P(), P("row", None)),
        out_specs=P("row", "col"),
        check_vma=False,
    )
```

```python
import jax
import jax.numpy as jnp
from jax import lax
from jax.experimental import pallas as pl
from jax.experimental.pallas import tpu as pltpu
from jax.sharding import PartitionSpec as P


TB = 512
VM = pl.BlockSpec(memory_space=pltpu.VMEM)
SM = pl.BlockSpec(memory_space=pltpu.SMEM)
HB = pl.BlockSpec(memory_space=pl.ANY)
F32 = jnp.float32
BF16 = jnp.bfloat16


def dot_t(a, b):
    return lax.dot_general(a, b, (((1,), (1,)), ((), ())), preferred_element_type=F32)


def bf(a):
    return a.astype(BF16)


def wendland(left, right):
    sq_dist = None
    for component in range(3):
        offset = left[:, component : component + 1] - right[component : component + 1, :]
        sq_dist = offset * offset if sq_dist is None else sq_dist + offset * offset
    radius = jnp.sqrt(sq_dist)
    falloff = jnp.maximum(1.0 - radius, 0.0)
    falloff = falloff * falloff
    return falloff * falloff * (4.0 * radius + 1.0)


def sites(tile, lengths, blocks, coords):
    start = pl.multiple_of(blocks[tile] * TB, TB)
    return jnp.concatenate([coords[c : c + 1, pl.ds(start, TB)] / lengths[c] for c in range(3)], axis=0)


def as_columns(parts):
    return jnp.concatenate([parts, jnp.zeros((5, TB), F32)], axis=0).T


def put(ref, at, to, left, right, kept):
    for s in range(0, TB, 64):
        ref[at + s : at + s + 64, to : to + TB] = wendland(left[s : s + 64], right) * kept.astype(F32)


def panels_kernel(row_tiles_n, row_count):
    def body(lengths, pattern, blocks, coords, inverses, cov_rows, cov_cols, cov_first, inverse):
        place_row, col_tile = place()
        panels = [sites(p, lengths, blocks, coords) for p in range(2)]
        for slot in range(row_tiles_n):
            tile = slot * row_count + place_row
            left = as_columns(sites(tile, lengths, blocks, coords))
            for p in range(2):
                put(cov_rows, slot * TB, p * TB, left, panels[p], pattern[tile, p])
        left = as_columns(sites(col_tile, lengths, blocks, coords))
        for p in range(2):
            put(cov_cols, 0, p * TB, left, panels[p], pattern[col_tile, p])
        put(cov_first, 0, 0, as_columns(panels[1]), panels[0], pattern[1, 0])
        for p in range(2):
            inverse[p] = bf(inverses[p])

    return body


def schur_kernel(row_tiles_n, row_count):
    def body(lengths, pattern, blocks, coords, cov_schur):
        place_row, col_tile = place()
        right = sites(col_tile, lengths, blocks, coords)
        for slot in range(row_tiles_n):
            tile = slot * row_count + place_row
            left = as_columns(sites(tile, lengths, blocks, coords))
            put(cov_schur, slot * TB, 0, left, right, pattern[tile, col_tile])

    return body


def fetch(pairs, sems):
    copies = [pltpu.make_async_copy(source, to, sems.at[n]) for n, (source, to) in enumerate(pairs)]
    for copy in copies:
        copy.start()
    return copies


def place():
    row = lax.axis_index("row")
    col = lax.axis_index("col")
    return row, col


def pack_kernel(parts):
    def body(earlier, out, staged, sems, out_sems):
        row, col = place()
        count = out.shape[0]
        start = jnp.where(row == col % count, col // count * count, 0)
        each = count // parts
        steps = [n * each for n in range(parts)]
        copies = fetch([(earlier.at[pl.ds(start + s, each)], staged.at[pl.ds(s, each)]) for s in steps], sems)
        outs = []
        for n, s in enumerate(steps):
            copies[n].wait()
            outs += fetch([(staged.at[pl.ds(s, each)], out.at[pl.ds(s, each)])], out_sems.at[pl.ds(n, 1)])
        for copy in outs:
            copy.wait()

    return body


def spread_kernel(scattered, out, piece, sems, out_sems):
    _, col = place()
    count = out.shape[0]
    for copy in fetch([(scattered.at[col % count], piece)], sems):
        copy.wait()
    for copy in fetch([(piece, out.at[n]) for n in range(count)], out_sems):
        copy.wait()


def times_inverse(block, inverse):
    block = bf(block)
    half = TB // 2
    left = dot_t(block[:, :half], inverse[:half, :half])
    return bf(jnp.concatenate([left, dot_t(block, inverse[half:])], axis=1))


def panel_parts(own, other, panels):
    core = place()[1] % 2
    return [(own, panels.at[1 - core]), (other, panels.at[core])]


def rows_kernel(chunk):
    def body(
        own, other, earlier, cov_rows_in, cov_first_in, inverse_in, first, second, first_tile,
        panels, rows, cov_rows, cov_first, inverse, sems,
    ):
        steps = [pl.ds(s, chunk) for s in range(0, rows.shape[0], chunk)]
        pairs = panel_parts(own, other, panels) + [(cov_first_in, cov_first), (inverse_in, inverse)]
        for at in steps:
            pairs += [(earlier.at[at], rows.at[at]), (cov_rows_in.at[at], cov_rows.at[at])]
        copies = fetch(pairs, sems)
        for copy in copies[:2]:
            copy.wait()
        zero = panels[0].reshape(TB, -1)
        one = panels[1].reshape(TB, -1)
        tile = dot_t(one, zero)
        for copy in copies[2:4]:
            copy.wait()
        tile = times_inverse(cov_first[...] - tile, inverse[0])
        first_tile[...] = tile
        for n, at in enumerate(steps):
            for copy in copies[4 + 2 * n : 6 + 2 * n]:
                copy.wait()
            block = rows[at]
            got = times_inverse(cov_rows[at, :TB] - dot_t(block, zero), inverse[0])
            first[at] = got
            rest = cov_rows[at, TB:] - dot_t(block, one) - dot_t(got, tile)
            second[at] = times_inverse(rest, inverse[1])

    return body


def tail_kernel(chunk):
    def body(
        column_in, own, other, earlier, cov_schur_in, cov_cols_in, inverse_in, first_in, second_in, first_tile_in, out,
        column, panels, rows, cov_schur, cov_cols, inverse, first, second, first_tile, result, sems, out_sems,
    ):
        steps = [pl.ds(s, chunk) for s in range(0, rows.shape[0], chunk)]
        count = len(steps)
        pairs = [(column_in, column)] + [(earlier.at[at], rows.at[at]) for at in steps]
        pairs += panel_parts(own, other, panels) + [(cov_cols_in, cov_cols), (inverse_in, inverse)]
        pairs += [(first_tile_in, first_tile), (first_in, first), (second_in, second), (cov_schur_in, cov_schur)]
        copies = fetch(pairs, sems)
        copies[0].wait()
        mine = column[...].reshape(TB, -1)
        for n, at in enumerate(steps):
            copies[1 + n].wait()
            result[at] = dot_t(rows[at], mine)
        for copy in copies[1 + count : -3]:
            copy.wait()
        start = cov_cols[:, :TB] - dot_t(mine, panels[0].reshape(TB, -1))
        col_first = times_inverse(start, inverse[0])
        rest = cov_cols[:, TB:] - dot_t(mine, panels[1].reshape(TB, -1)) - dot_t(col_first, first_tile[...])
        col_second = times_inverse(rest, inverse[1])
        for copy in copies[-3:]:
            copy.wait()
        outs = []
        for n, at in enumerate(steps):
            result[at] = cov_schur[at] - result[at] - dot_t(first[at], col_first) - dot_t(second[at], col_second)
            outs += fetch([(result.at[at], out.at[at])], out_sems.at[pl.ds(n, 1)])
        for copy in outs:
            copy.wait()

    return body


def call(body, outs, specs, out_specs=None, limit=63, **kw):
    return pl.pallas_call(
        body,
        out_shape=outs,
        in_specs=specs,
        out_specs=out_specs or [VM] * len(outs),
        compiler_params=pltpu.CompilerParams(vmem_limit_bytes=limit * 1024 * 1024),
        **kw,
    )


def steps(coords, lengths, pattern, blocks, inverses, earlier):
    row_count = lax.axis_size("row")
    col_count = lax.axis_size("col")
    rows_n, width = earlier.shape
    row_tiles_n = rows_n // TB
    piece = TB // row_count
    dma = pltpu.SemaphoreType.DMA

    pieces = (row_count, piece, width)
    tile_buffer = pltpu.VMEM(pieces, BF16)
    mine = call(
        pack_kernel(4),
        jax.ShapeDtypeStruct(pieces, BF16),
        [HB],
        HB,
        scratch_shapes=[tile_buffer, dma((4,)), dma((4,))],
        name="pack",
    )(earlier.reshape(-1, piece, width))
    scattered = lax.all_to_all(mine, "row", 0, 0)
    (cov_schur,) = call(
        schur_kernel(row_tiles_n, row_count),
        [jax.ShapeDtypeStruct((rows_n, TB), F32)],
        [SM, SM, SM, VM],
        name="schur",
    )(lengths, pattern, blocks, coords)
    scattered, cov_schur, later = lax.optimization_barrier((scattered, cov_schur, lengths))
    panel_piece = lax.dynamic_index_in_dim(scattered, 1 - lax.axis_index("col") % 2, 0, keepdims=True)
    own = lax.all_to_all(jnp.broadcast_to(panel_piece, pieces), "row", 0, 0)
    spread = call(
        spread_kernel,
        jax.ShapeDtypeStruct(pieces, BF16),
        [HB],
        HB,
        scratch_shapes=[pltpu.VMEM((piece, width), BF16), dma((1,)), dma((row_count,))],
        name="spread",
    )(scattered)
    cov_rows, cov_cols, cov_first, inverse = call(
        panels_kernel(row_tiles_n, row_count),
        [
            jax.ShapeDtypeStruct((rows_n, 2 * TB), F32),
            jax.ShapeDtypeStruct((TB, 2 * TB), F32),
            jax.ShapeDtypeStruct((TB, TB), F32),
            jax.ShapeDtypeStruct((2, TB, TB), BF16),
        ],
        [SM, SM, SM, VM, VM],
        name="panels",
    )(later, pattern, blocks, coords, inverses)
    own, spread, cov_rows = lax.optimization_barrier((own, spread, cov_rows))
    column = lax.all_to_all(spread, "row", 0, 0)
    other = lax.ppermute(own, "col", [(c, c ^ 1) for c in range(col_count)])
    chunk = 256
    count = rows_n // chunk
    panels = pltpu.VMEM((2,) + pieces, BF16)
    square = pltpu.VMEM((TB, TB), BF16)
    pair = pltpu.VMEM((2, TB, TB), BF16)
    tall = pltpu.VMEM((rows_n, TB), BF16)
    whole = pltpu.VMEM(earlier.shape, BF16)
    block = pltpu.VMEM((rows_n, TB), F32)
    first, second, first_tile = call(
        rows_kernel(chunk),
        [
            jax.ShapeDtypeStruct((rows_n, TB), BF16),
            jax.ShapeDtypeStruct((rows_n, TB), BF16),
            jax.ShapeDtypeStruct((TB, TB), BF16),
        ],
        [HB] * 6,
        scratch_shapes=[
            panels, whole, pltpu.VMEM((rows_n, 2 * TB), F32), pltpu.VMEM((TB, TB), F32), pair, dma((4 + 2 * count,)),
        ],
        name="rows",
    )(own, other, earlier, cov_rows, cov_first, inverse)
    return call(
        tail_kernel(chunk),
        jax.ShapeDtypeStruct((rows_n, TB), F32),
        [HB] * 10,
        HB,
        scratch_shapes=[
            tile_buffer, panels, whole, block, pltpu.VMEM((TB, 2 * TB), F32), pair, tall, tall, square, block,
            dma((9 + count,)), dma((count,)),
        ],
        name="tail",
    )(column, own, other, earlier, cov_schur, cov_cols, inverse, first, second, first_tile)


def solution(mesh):
    return jax.shard_map(
        steps,
        mesh=mesh,
        in_specs=(P(), P(), P(), P(), P(), P("row", None)),
        out_specs=P("row", "col"),
        check_vma=False,
    )
```

```python
import jax
import jax.numpy as jnp
from jax import lax
from jax.experimental import pallas as pl
from jax.experimental.pallas import tpu as pltpu
from jax.sharding import PartitionSpec as P


TB = 512
VM = pl.BlockSpec(memory_space=pltpu.VMEM)
SM = pl.BlockSpec(memory_space=pltpu.SMEM)
HB = pl.BlockSpec(memory_space=pl.ANY)
F32 = jnp.float32
BF16 = jnp.bfloat16


def dot_t(a, b):
    return lax.dot_general(a, b, (((1,), (1,)), ((), ())), preferred_element_type=F32)


def bf(a):
    return a.astype(BF16)


def wendland(left, right):
    sq_dist = None
    for component in range(3):
        offset = left[:, component : component + 1] - right[component : component + 1, :]
        sq_dist = offset * offset if sq_dist is None else sq_dist + offset * offset
    radius = jnp.sqrt(sq_dist)
    falloff = jnp.maximum(1.0 - radius, 0.0)
    falloff = falloff * falloff
    return falloff * falloff * (4.0 * radius + 1.0)


def sites(tile, lengths, blocks, coords):
    start = pl.multiple_of(blocks[tile] * TB, TB)
    return jnp.concatenate([coords[c : c + 1, pl.ds(start, TB)] / lengths[c] for c in range(3)], axis=0)


def as_columns(parts):
    return jnp.concatenate([parts, jnp.zeros((5, TB), F32)], axis=0).T


def put(ref, at, to, left, right, kept):
    for s in range(0, TB, 64):
        ref[at + s : at + s + 64, to : to + TB] = wendland(left[s : s + 64], right) * kept.astype(F32)


def cols_kernel(lengths, pattern, blocks, coords, inverses, cov_cols, inverse):
    col_tile = place()[1]
    left = as_columns(sites(col_tile, lengths, blocks, coords))
    for p in range(2):
        put(cov_cols, 0, p * TB, left, sites(p, lengths, blocks, coords), pattern[col_tile, p])
        inverse[p] = bf(inverses[p])


def panels_kernel(row_tiles_n, row_count):
    def body(lengths, pattern, blocks, coords, cov_rows, cov_first):
        place_row = place()[0]
        panels = [sites(p, lengths, blocks, coords) for p in range(2)]
        for slot in range(row_tiles_n):
            tile = slot * row_count + place_row
            left = as_columns(sites(tile, lengths, blocks, coords))
            for p in range(2):
                put(cov_rows, slot * TB, p * TB, left, panels[p], pattern[tile, p])
        put(cov_first, 0, 0, as_columns(panels[1]), panels[0], pattern[1, 0])

    return body


def schur_kernel(row_tiles_n, row_count):
    def body(lengths, pattern, blocks, coords, cov_schur):
        place_row, col_tile = place()
        right = sites(col_tile, lengths, blocks, coords)
        for slot in range(row_tiles_n):
            tile = slot * row_count + place_row
            left = as_columns(sites(tile, lengths, blocks, coords))
            put(cov_schur, slot * TB, 0, left, right, pattern[tile, col_tile])

    return body


def fetch(pairs, sems):
    copies = [pltpu.make_async_copy(source, to, sems.at[n]) for n, (source, to) in enumerate(pairs)]
    for copy in copies:
        copy.start()
    return copies


def place():
    row = lax.axis_index("row")
    col = lax.axis_index("col")
    return row, col


def pack_kernel(parts):
    def body(earlier, out, staged, sems, out_sems):
        row, col = place()
        count = out.shape[0]
        held = jnp.logical_and(row // 2 == col % count // 2, col >= count + 2)
        start = jnp.where(held, 2 * count, 0) + col % 2 * count
        each = count // parts
        steps = [n * each for n in range(parts)]
        copies = fetch([(earlier.at[pl.ds(start + s, each)], staged.at[pl.ds(s, each)]) for s in steps], sems)
        outs = []
        for n, s in enumerate(steps):
            copies[n].wait()
            outs += fetch([(staged.at[pl.ds(s, each)], out.at[pl.ds(s, each)])], out_sems.at[pl.ds(n, 1)])
        for copy in outs:
            copy.wait()

    return body


def spread_kernel(scattered, exchanged, planed, out, piece, sems, out_sems):
    _, col = place()
    count = out.shape[0]
    core = col % 2
    clash = col // 2 == count // 2

    @pl.when(clash)
    def _():
        for copy in fetch([(planed.at[h], piece.at[h]) for h in range(2)], sems):
            copy.wait()

    @pl.when(jnp.logical_not(clash))
    def _():
        for copy in fetch([(scattered.at[col % count], piece.at[core]), (exchanged.at[0], piece.at[1 - core])], sems):
            copy.wait()

    for copy in fetch([(piece, out.at[n]) for n in range(count)], out_sems):
        copy.wait()


def times_inverse(block, inverse):
    block = bf(block)
    half = TB // 2
    left = dot_t(block[:, :half], inverse[:half, :half])
    return bf(jnp.concatenate([left, dot_t(block, inverse[half:])], axis=1))


def panel_parts(own, other, panels):
    core = place()[1] % 2
    pairs = []
    for p in range(2):
        pairs += [(own.at[:, p], panels.at[p, core]), (other.at[:, p], panels.at[p, 1 - core])]
    return pairs


def rows_kernel(chunk):
    def body(
        own, other, earlier, cov_rows_in, cov_first_in, inverse_in, first, second, first_tile,
        panels, rows, cov_rows, cov_first, inverse, sems,
    ):
        steps = [pl.ds(s, chunk) for s in range(0, rows.shape[0], chunk)]
        pairs = panel_parts(own, other, panels) + [(cov_first_in, cov_first), (inverse_in, inverse)]
        for at in steps:
            pairs += [(earlier.at[at], rows.at[at]), (cov_rows_in.at[at], cov_rows.at[at])]
        copies = fetch(pairs, sems)
        for copy in copies[:4]:
            copy.wait()
        zero = panels[0].reshape(TB, -1)
        one = panels[1].reshape(TB, -1)
        tile = dot_t(one, zero)
        for copy in copies[4:6]:
            copy.wait()
        tile = times_inverse(cov_first[...] - tile, inverse[0])
        first_tile[...] = tile
        for n, at in enumerate(steps):
            for copy in copies[6 + 2 * n : 8 + 2 * n]:
                copy.wait()
            block = rows[at]
            got = times_inverse(cov_rows[at, :TB] - dot_t(block, zero), inverse[0])
            first[at] = got
            rest = cov_rows[at, TB:] - dot_t(block, one) - dot_t(got, tile)
            second[at] = times_inverse(rest, inverse[1])

    return body


def tail_kernel(chunk):
    def body(
        column_in, own, other, earlier, cov_schur_in, cov_cols_in, inverse_in, first_in, second_in, first_tile_in, out,
        column, panels, rows, cov_schur, cov_cols, inverse, first, second, first_tile, result, sems, out_sems,
    ):
        steps = [pl.ds(s, chunk) for s in range(0, rows.shape[0], chunk)]
        count = len(steps)
        pairs = [(column_in.at[:, h], column.at[h]) for h in range(2)]
        pairs += [(earlier.at[at], rows.at[at]) for at in steps]
        pairs += panel_parts(own, other, panels) + [(cov_cols_in, cov_cols), (inverse_in, inverse)]
        pairs += [(first_tile_in, first_tile), (first_in, first), (second_in, second), (cov_schur_in, cov_schur)]
        copies = fetch(pairs, sems)
        for copy in copies[:2]:
            copy.wait()
        mine = column[...].reshape(TB, -1)
        for n, at in enumerate(steps):
            copies[2 + n].wait()
            result[at] = dot_t(rows[at], mine)
        for copy in copies[2 + count : -3]:
            copy.wait()
        start = cov_cols[:, :TB] - dot_t(mine, panels[0].reshape(TB, -1))
        col_first = times_inverse(start, inverse[0])
        rest = cov_cols[:, TB:] - dot_t(mine, panels[1].reshape(TB, -1)) - dot_t(col_first, first_tile[...])
        col_second = times_inverse(rest, inverse[1])
        for copy in copies[-3:]:
            copy.wait()
        outs = []
        for n, at in enumerate(steps):
            result[at] = cov_schur[at] - result[at] - dot_t(first[at], col_first) - dot_t(second[at], col_second)
            outs += fetch([(result.at[at], out.at[at])], out_sems.at[pl.ds(n, 1)])
        for copy in outs:
            copy.wait()

    return body


def call(body, outs, specs, out_specs=None, limit=63, **kw):
    return pl.pallas_call(
        body,
        out_shape=outs,
        in_specs=specs,
        out_specs=out_specs or [VM] * len(outs),
        compiler_params=pltpu.CompilerParams(vmem_limit_bytes=limit * 1024 * 1024),
        **kw,
    )


def steps(coords, lengths, pattern, blocks, inverses, earlier):
    row_count = lax.axis_size("row")
    col_count = lax.axis_size("col")
    rows_n, width = earlier.shape
    row_tiles_n = rows_n // TB
    piece = TB // row_count
    dma = pltpu.SemaphoreType.DMA

    half = piece // 2
    pieces = (row_count, half, width)
    both = (row_count, 2, half, width)
    halves = earlier.reshape(-1, half, width)
    mine = call(
        pack_kernel(2),
        jax.ShapeDtypeStruct(pieces, BF16),
        [HB],
        HB,
        scratch_shapes=[pltpu.VMEM(pieces, BF16), dma((2,)), dma((2,))],
        name="pack",
    )(halves)
    scattered = lax.all_to_all(mine, "row", 0, 0)
    col_index = lax.axis_index("col")
    first_col = row_count // 2
    to_row = jnp.clip(col_index - first_col, 0, row_count - 1)
    planed = lax.dynamic_slice_in_dim(halves.reshape(2, 2, row_count, half, width)[1], to_row, 1, 1)
    planed = lax.ppermute(
        planed,
        ("row", "col"),
        [(t * col_count + first_col + r, r * col_count + row_count + t) for t in range(2) for r in range(row_count)],
    )
    (cov_schur,) = call(
        schur_kernel(row_tiles_n, row_count),
        [jax.ShapeDtypeStruct((rows_n, TB), F32)],
        [SM, SM, SM, VM],
        name="schur",
    )(lengths, pattern, blocks, coords)
    cov_cols, inverse = call(
        cols_kernel,
        [jax.ShapeDtypeStruct((TB, 2 * TB), F32), jax.ShapeDtypeStruct((2, TB, TB), BF16)],
        [SM, SM, SM, VM, VM],
        name="cols",
    )(lengths, pattern, blocks, coords, inverses)
    scattered, cov_schur, cov_cols, later = lax.optimization_barrier((scattered, cov_schur, cov_cols, lengths))
    own = lax.all_to_all(jnp.broadcast_to(scattered[:2], both), "row", 0, 0)
    partner = [(c, c ^ 1) for c in range(col_count)]
    theirs = lax.dynamic_slice_in_dim(scattered, (col_index ^ 1) % row_count, 1, 0)
    exchanged = lax.ppermute(theirs, "col", partner)
    cov_rows, cov_first = call(
        panels_kernel(row_tiles_n, row_count),
        [jax.ShapeDtypeStruct((rows_n, 2 * TB), F32), jax.ShapeDtypeStruct((TB, TB), F32)],
        [SM, SM, SM, VM],
        name="panels",
    )(later, pattern, blocks, coords)
    spread = call(
        spread_kernel,
        jax.ShapeDtypeStruct(both, BF16),
        [HB] * 3,
        HB,
        scratch_shapes=[pltpu.VMEM(both[1:], BF16), dma((2,)), dma((row_count,))],
        name="spread",
    )(scattered, exchanged, planed.reshape(both[1:]))
    own, spread, cov_rows = lax.optimization_barrier((own, spread, cov_rows))
    column = lax.all_to_all(spread, "row", 0, 0)
    other = lax.ppermute(own, "col", partner)
    chunk = 256
    count = rows_n // chunk
    panels = pltpu.VMEM((2, 2) + pieces, BF16)
    square = pltpu.VMEM((TB, TB), BF16)
    pair = pltpu.VMEM((2, TB, TB), BF16)
    tall = pltpu.VMEM((rows_n, TB), BF16)
    whole = pltpu.VMEM(earlier.shape, BF16)
    block = pltpu.VMEM((rows_n, TB), F32)
    first, second, first_tile = call(
        rows_kernel(chunk),
        [
            jax.ShapeDtypeStruct((rows_n, TB), BF16),
            jax.ShapeDtypeStruct((rows_n, TB), BF16),
            jax.ShapeDtypeStruct((TB, TB), BF16),
        ],
        [HB] * 6,
        scratch_shapes=[
            panels, whole, pltpu.VMEM((rows_n, 2 * TB), F32), pltpu.VMEM((TB, TB), F32), pair, dma((6 + 2 * count,)),
        ],
        name="rows",
    )(own, other, earlier, cov_rows, cov_first, inverse)
    return call(
        tail_kernel(chunk),
        jax.ShapeDtypeStruct((rows_n, TB), F32),
        [HB] * 10,
        HB,
        scratch_shapes=[
            pltpu.VMEM((2,) + pieces, BF16), panels, whole, block, pltpu.VMEM((TB, 2 * TB), F32), pair, tall, tall, square, block,
            dma((12 + count,)), dma((count,)),
        ],
        name="tail",
    )(column, own, other, earlier, cov_schur, cov_cols, inverse, first, second, first_tile)


def solution(mesh):
    return jax.shard_map(
        steps,
        mesh=mesh,
        in_specs=(P(), P(), P(), P(), P(), P("row", None)),
        out_specs=P("row", "col"),
        check_vma=False,
    )
```

```python
import jax
import jax.numpy as jnp
from jax import lax
from jax.experimental import pallas as pl
from jax.experimental.pallas import tpu as pltpu
from jax.sharding import PartitionSpec as P


TB = 512
VM = pl.BlockSpec(memory_space=pltpu.VMEM)
SM = pl.BlockSpec(memory_space=pltpu.SMEM)
HB = pl.BlockSpec(memory_space=pl.ANY)
F32 = jnp.float32
BF16 = jnp.bfloat16


def dot_t(a, b):
    return lax.dot_general(a, b, (((1,), (1,)), ((), ())), preferred_element_type=F32)


def bf(a):
    return a.astype(BF16)


def wendland(left, right):
    sq_dist = None
    for component in range(3):
        offset = left[:, component : component + 1] - right[component : component + 1, :]
        sq_dist = offset * offset if sq_dist is None else sq_dist + offset * offset
    radius = jnp.sqrt(sq_dist)
    falloff = jnp.maximum(1.0 - radius, 0.0)
    falloff = falloff * falloff
    return falloff * falloff * (4.0 * radius + 1.0)


def sites(tile, lengths, blocks, coords):
    start = pl.multiple_of(blocks[tile] * TB, TB)
    return jnp.concatenate([coords[c : c + 1, pl.ds(start, TB)] / lengths[c] for c in range(3)], axis=0)


def as_columns(parts):
    return jnp.concatenate([parts, jnp.zeros((5, TB), F32)], axis=0).T


def put(ref, at, to, left, right, kept):
    for s in range(0, TB, 64):
        ref[at + s : at + s + 64, to : to + TB] = wendland(left[s : s + 64], right) * kept.astype(F32)


def cols_kernel(lengths, pattern, blocks, coords, cov_cols):
    col_tile = place()[1]
    left = as_columns(sites(col_tile, lengths, blocks, coords))
    for p in range(2):
        put(cov_cols, 0, p * TB, left, sites(p, lengths, blocks, coords), pattern[col_tile, p])


def panels_kernel(row_tiles_n, row_count):
    def body(lengths, pattern, blocks, coords, cov_rows, cov_first):
        place_row = place()[0]
        panels = [sites(p, lengths, blocks, coords) for p in range(2)]
        for slot in range(row_tiles_n):
            tile = slot * row_count + place_row
            left = as_columns(sites(tile, lengths, blocks, coords))
            for p in range(2):
                put(cov_rows, slot * TB, p * TB, left, panels[p], pattern[tile, p])
        put(cov_first, 0, 0, as_columns(panels[1]), panels[0], pattern[1, 0])

    return body


def schur_kernel(row_tiles_n, row_count):
    def body(lengths, pattern, blocks, coords, cov_schur):
        place_row, col_tile = place()
        right = sites(col_tile, lengths, blocks, coords)
        for slot in range(row_tiles_n):
            tile = slot * row_count + place_row
            left = as_columns(sites(tile, lengths, blocks, coords))
            put(cov_schur, slot * TB, 0, left, right, pattern[tile, col_tile])

    return body


def fetch(pairs, sems):
    copies = [pltpu.make_async_copy(source, to, sems.at[n]) for n, (source, to) in enumerate(pairs)]
    for copy in copies:
        copy.start()
    return copies


def place():
    row = lax.axis_index("row")
    col = lax.axis_index("col")
    return row, col


def pack_kernel(parts):
    def body(earlier, out, staged, sems, out_sems):
        row, col = place()
        count = out.shape[0]
        held = jnp.logical_and(row // 2 == col % count // 2, col >= count)
        start = jnp.where(held, 2 * count, 0) + col % 2 * count
        each = count // parts
        steps = [n * each for n in range(parts)]
        copies = fetch([(earlier.at[pl.ds(start + s, each)], staged.at[pl.ds(s, each)]) for s in steps], sems)
        outs = []
        for n, s in enumerate(steps):
            copies[n].wait()
            outs += fetch([(staged.at[pl.ds(s, each)], out.at[pl.ds(s, each)])], out_sems.at[pl.ds(n, 1)])
        for copy in outs:
            copy.wait()

    return body


def spread_kernel(scattered, exchanged, out, piece, sems, out_sems):
    _, col = place()
    count = out.shape[0]
    core = col % 2
    for copy in fetch([(scattered.at[col % count], piece.at[core]), (exchanged.at[0], piece.at[1 - core])], sems):
        copy.wait()
    for copy in fetch([(piece, out.at[n]) for n in range(count)], out_sems):
        copy.wait()


def times_inverse(block, inverse):
    block = bf(block)
    half = TB // 2
    left = dot_t(block[:, :half], inverse[:half, :half])
    return bf(jnp.concatenate([left, dot_t(block, inverse[half:])], axis=1))


def panel_parts(own, other, panels):
    core = place()[1] % 2
    pairs = []
    for p in range(2):
        pairs += [(own.at[:, p], panels.at[p, core]), (other.at[:, p], panels.at[p, 1 - core])]
    return pairs


def rows_kernel(chunk):
    def body(
        own, other, earlier, cov_rows_in, cov_first_in, inverses_in, first_out, second_out, first_tile_out, inverse_out,
        panels, rows, cov_rows, cov_first, inverses, first, second, first_tile, inverse, sems, out_sems,
    ):
        steps = [pl.ds(s, chunk) for s in range(0, rows.shape[0], chunk)]
        pairs = panel_parts(own, other, panels) + [(inverses_in, inverses), (cov_first_in, cov_first)]
        for at in steps:
            pairs += [(earlier.at[at], rows.at[at]), (cov_rows_in.at[at], cov_rows.at[at])]
        copies = fetch(pairs, sems)
        outs = []

        def put_out(source, to):
            outs.extend(fetch([(source, to)], out_sems.at[pl.ds(len(outs), 1)]))

        for copy in copies[:4]:
            copy.wait()
        zero = panels[0].reshape(TB, -1)
        one = panels[1].reshape(TB, -1)
        tile = dot_t(one, zero)
        for copy in copies[4:6]:
            copy.wait()
        inverse[...] = bf(inverses[...])
        put_out(inverse, inverse_out)
        tile = times_inverse(cov_first[...] - tile, inverse[0])
        first_tile[...] = tile
        put_out(first_tile, first_tile_out)
        for n, at in enumerate(steps):
            for copy in copies[6 + 2 * n : 8 + 2 * n]:
                copy.wait()
            block = rows[at]
            got = times_inverse(cov_rows[at, :TB] - dot_t(block, zero), inverse[0])
            first[at] = got
            put_out(first.at[at], first_out.at[at])
            rest = cov_rows[at, TB:] - dot_t(block, one) - dot_t(got, tile)
            second[at] = times_inverse(rest, inverse[1])
            put_out(second.at[at], second_out.at[at])
        for copy in outs:
            copy.wait()

    return body


def tail_kernel(chunk):
    def body(
        column_in, own, other, earlier, cov_schur_in, cov_cols_in, inverse_in, first_in, second_in, first_tile_in, out,
        column, panels, rows, cov_schur, cov_cols, inverse, first, second, first_tile, result, sems, out_sems,
    ):
        steps = [pl.ds(s, chunk) for s in range(0, rows.shape[0], chunk)]
        count = len(steps)
        pairs = [(column_in.at[:, h], column.at[h]) for h in range(2)]
        pairs += [(earlier.at[at], rows.at[at]) for at in steps]
        pairs += panel_parts(own, other, panels) + [(cov_cols_in, cov_cols), (inverse_in, inverse)]
        pairs += [(first_tile_in, first_tile), (first_in, first), (second_in, second), (cov_schur_in, cov_schur)]
        copies = fetch(pairs, sems)
        for copy in copies[:2]:
            copy.wait()
        mine = column[...].reshape(TB, -1)
        for n, at in enumerate(steps):
            copies[2 + n].wait()
            result[at] = dot_t(rows[at], mine)
        for copy in copies[2 + count : -3]:
            copy.wait()
        start = cov_cols[:, :TB] - dot_t(mine, panels[0].reshape(TB, -1))
        col_first = times_inverse(start, inverse[0])
        rest = cov_cols[:, TB:] - dot_t(mine, panels[1].reshape(TB, -1)) - dot_t(col_first, first_tile[...])
        col_second = times_inverse(rest, inverse[1])
        for copy in copies[-3:]:
            copy.wait()
        outs = []
        for n, at in enumerate(steps):
            result[at] = cov_schur[at] - result[at] - dot_t(first[at], col_first) - dot_t(second[at], col_second)
            outs += fetch([(result.at[at], out.at[at])], out_sems.at[pl.ds(n, 1)])
        for copy in outs:
            copy.wait()

    return body


def call(body, outs, specs, out_specs=None, limit=63, **kw):
    return pl.pallas_call(
        body,
        out_shape=outs,
        in_specs=specs,
        out_specs=out_specs or [VM] * len(outs),
        compiler_params=pltpu.CompilerParams(vmem_limit_bytes=limit * 1024 * 1024),
        **kw,
    )


def steps(coords, lengths, pattern, blocks, inverses, earlier):
    row_count = lax.axis_size("row")
    col_count = lax.axis_size("col")
    rows_n, width = earlier.shape
    row_tiles_n = rows_n // TB
    piece = TB // row_count
    dma = pltpu.SemaphoreType.DMA

    half = piece // 2
    pieces = (row_count, half, width)
    both = (row_count, 2, half, width)
    halves = earlier.reshape(-1, half, width)
    mine = call(
        pack_kernel(2),
        jax.ShapeDtypeStruct(pieces, BF16),
        [HB],
        HB,
        scratch_shapes=[pltpu.VMEM(pieces, BF16), dma((2,)), dma((2,))],
        name="pack",
    )(halves)
    scattered = lax.all_to_all(mine, "row", 0, 0)
    col_index = lax.axis_index("col")
    (cov_schur,) = call(
        schur_kernel(row_tiles_n, row_count),
        [jax.ShapeDtypeStruct((rows_n, TB), F32)],
        [SM, SM, SM, VM],
        name="schur",
    )(lengths, pattern, blocks, coords)
    (cov_cols,) = call(
        cols_kernel, [jax.ShapeDtypeStruct((TB, 2 * TB), F32)], [SM, SM, SM, VM], name="cols"
    )(lengths, pattern, blocks, coords)
    scattered, cov_schur, cov_cols, later = lax.optimization_barrier((scattered, cov_schur, cov_cols, lengths))
    panel_piece = scattered[:2]
    passed = lax.ppermute(
        panel_piece,
        ("row", "col"),
        [(r * col_count + row_count + 2 + k, r * col_count + row_count + k) for r in range(row_count) for k in range(2)],
    )
    panel_piece = jnp.where(col_index // 2 == row_count // 2, passed, panel_piece)
    own = lax.all_to_all(jnp.broadcast_to(panel_piece, both), "row", 0, 0)
    partner = [(c, c ^ 1) for c in range(col_count)]
    theirs = lax.dynamic_slice_in_dim(scattered, (col_index ^ 1) % row_count, 1, 0)
    exchanged = lax.ppermute(theirs, "col", partner)
    cov_rows, cov_first = call(
        panels_kernel(row_tiles_n, row_count),
        [jax.ShapeDtypeStruct((rows_n, 2 * TB), F32), jax.ShapeDtypeStruct((TB, TB), F32)],
        [SM, SM, SM, VM],
        name="panels",
    )(later, pattern, blocks, coords)
    spread = call(
        spread_kernel,
        jax.ShapeDtypeStruct(both, BF16),
        [HB] * 2,
        HB,
        scratch_shapes=[pltpu.VMEM(both[1:], BF16), dma((2,)), dma((row_count,))],
        name="spread",
    )(scattered, exchanged)
    own, spread, cov_rows = lax.optimization_barrier((own, spread, cov_rows))
    column = lax.all_to_all(spread, "row", 0, 0)
    other = lax.ppermute(own, "col", partner)
    chunk = 256
    count = rows_n // chunk
    panels = pltpu.VMEM((2, 2) + pieces, BF16)
    square = pltpu.VMEM((TB, TB), BF16)
    pair = pltpu.VMEM((2, TB, TB), BF16)
    tall = pltpu.VMEM((rows_n, TB), BF16)
    whole = pltpu.VMEM(earlier.shape, BF16)
    block = pltpu.VMEM((rows_n, TB), F32)
    first, second, first_tile, inverse = call(
        rows_kernel(chunk),
        [
            jax.ShapeDtypeStruct((rows_n, TB), BF16),
            jax.ShapeDtypeStruct((rows_n, TB), BF16),
            jax.ShapeDtypeStruct((TB, TB), BF16),
            jax.ShapeDtypeStruct((2, TB, TB), BF16),
        ],
        [HB] * 6,
        [HB] * 4,
        scratch_shapes=[
            panels, whole, pltpu.VMEM((rows_n, 2 * TB), F32), pltpu.VMEM((TB, TB), F32),
            pltpu.VMEM((2, TB, TB), F32), tall, tall, square, pair, dma((6 + 2 * count,)), dma((2 + 2 * count,)),
        ],
        name="rows",
    )(own, other, earlier, cov_rows, cov_first, inverses)
    return call(
        tail_kernel(chunk),
        jax.ShapeDtypeStruct((rows_n, TB), F32),
        [HB] * 10,
        HB,
        scratch_shapes=[
            pltpu.VMEM((2,) + pieces, BF16), panels, whole, block, pltpu.VMEM((TB, 2 * TB), F32), pair, tall, tall, square, block,
            dma((12 + count,)), dma((count,)),
        ],
        name="tail",
    )(column, own, other, earlier, cov_schur, cov_cols, inverse, first, second, first_tile)


def solution(mesh):
    return jax.shard_map(
        steps,
        mesh=mesh,
        in_specs=(P(), P(), P(), P(), P(), P("row", None)),
        out_specs=P("row", "col"),
        check_vma=False,
    )
```
